32 devices in a mesh: rep: 4 (over y, x), shard: 8 (over z, core).
Axes of the slice: x: 2, y: 2, z: 4, core: 2. Of those that a mesh axis runs over, the one named last changes fastest.
Arguments:
- inputs: bfloat16 [32768, 1024], P(('rep', 'shard')), may hold values from -6 to 6
- query_weight: bfloat16 [1024, 256], P('shard'), may hold values from -0.1875 to 0.1875
- key_weight: bfloat16 [1024, 256], P('shard'), may hold values from -0.1875 to 0.1875
- value_weight: bfloat16 [1024, 1024], P('shard'), may hold values from -0.1875 to 0.1875
- out_weight: bfloat16 [1024, 1024], P('shard'), may hold values from -6 to 6
- gate_weight: bfloat16 [1024, 2752], P('shard'), may hold values from -0.1875 to 0.1875
- up_weight: bfloat16 [1024, 2752], P('shard'), may hold values from -0.1875 to 0.1875
- down_weight: bfloat16 [1024, 2752], P('shard'), may hold values from -0.109375 to 0.109375
- attn_gain: bfloat16 [1024], P('shard'), may hold values from 0.25 to 1.75
- mlp_gain: bfloat16 [1024], P('shard'), may hold values from 0.25 to 1.75
- slot_of: int32 [4, 8], P('rep'), may hold values from 0 to 7, each once within a row
- parent_of: int32 [4, 8], P('rep'), may hold values from 0 to 1, as said below
- cotangent: bfloat16 [32768, 1024], P(('rep', 'shard')), may hold values from -6 to 6
Outputs:
- block_out: bfloat16 [32768, 1024], P(('rep', 'shard'))
- input_grad: float32 [32768, 1024], P(('rep', 'shard'))
- query_grad: float32 [1024, 256], P('shard')
- key_grad: float32 [1024, 256], P('shard')
- value_grad: float32 [1024, 1024], P('shard')
- out_grad: float32 [1024, 1024], P('shard')
- gate_grad: float32 [1024, 2752], P('shard')
- up_grad: float32 [1024, 2752], P('shard')
- down_grad: float32 [1024, 2752], P('shard')
- attn_gain_grad: float32 [1024], P('shard')
- mlp_gain_grad: float32 [1024], P('shard')
The draws below stay inside these ranges and needn't reach their ends.
Inputs may be any that keep to these rules, and one draw needn't show every extreme that they name: `slot_of`: each row is a permutation of the slots of its group. `parent_of`: each row names each of the 2 families for exactly 4 continuations.
All inputs are finite; a program needn't handle non-finite values.
Results may differ from the reference program's by a relative error of at most 0.02.
Values may be sent and summed in bfloat16 or wider, within the bound.
No kernel may reach another device: no remote copies, remote signals or barrier semaphores. Data moves between devices by JAX's collectives and lax.ppermute only.
A program may use at most 320 MiB of HBM per device.

```python
import math
import jax
import jax.numpy as jnp
from jax import lax

D = 1024
HEADS = 16
FEAT = 16
DV = 64
FF = 2752
SEG = 512
CONT_PER = 4
TAYLOR = 273
TOK_DEV = 1024
PLEN = 2048
FAM_LEN = 4096
GROUPS = 4
SLOTS = 8
FAMILIES = 2
PIECES = 2
PIECE_SLOTS = 4
TOKENS = 32768


def draw_parent_of(key, part):
    row_keys = jax.random.split(jax.random.fold_in(key, 7), GROUPS)
    orders = jax.vmap(lambda row_key: jax.random.permutation(row_key, FAMILIES * CONT_PER))(row_keys)
    return (orders // CONT_PER).astype(jnp.int32)


def block_scale(stream_key, shape, shards, smallest, largest):
    def one(dim, parts):
        steps = jax.random.uniform(jax.random.fold_in(jax.random.fold_in(stream_key, 6), dim), (parts,), jnp.float32, smallest / len(shards), largest / len(shards))
        return jnp.repeat(jnp.exp(steps), shape[dim] // parts).reshape((-1,) + (1,) * (len(shape) - dim - 1))

    loudness = one(*shards[0])
    for cut in shards[1:]:
        loudness = loudness * one(*cut)
    return loudness


def centred(key, shape, deviation, reach, pieces=(), held_as=jnp.bfloat16):
    loudness = block_scale(key, shape, pieces, -0.22, 0.18) if pieces else 1.0
    values = jax.random.normal(key, shape, jnp.float32) * deviation * loudness
    return jnp.minimum(jnp.maximum(values, -reach), reach).astype(held_as)


def setup_inputs(seed: int = 0) -> dict:
    key_of = jax.random.split(jax.random.key(seed), 14)
    return {
        "inputs": centred(key_of[0], (TOKENS, D), 1.0, 6.0, ((0, 32),)),
        "query_weight": centred(key_of[1], (D, HEADS * FEAT), D ** -0.5, 0.1875, ((0, 8),)),
        "key_weight": centred(key_of[2], (D, HEADS * FEAT), D ** -0.5, 0.1875, ((0, 8),)),
        "value_weight": centred(key_of[3], (D, HEADS * DV), D ** -0.5, 0.1875, ((0, 8),)),
        "out_weight": centred(key_of[4], (D, HEADS * DV), (max(1, D // (2 * PLEN))) ** -0.5, 6.0, ((0, 8),)),
        "gate_weight": centred(key_of[5], (D, FF), D ** -0.5, 0.1875, ((0, 8),)),
        "up_weight": centred(key_of[6], (D, FF), D ** -0.5, 0.1875, ((0, 8),)),
        "down_weight": centred(key_of[7], (D, FF), FF ** -0.5, 0.109375, ((0, 8),)),
        "attn_gain": jnp.clip(1.0 + 0.15 * jax.random.normal(key_of[8], (D,), jnp.float32), 0.25, 1.75).astype(jnp.bfloat16),
        "mlp_gain": jnp.clip(1.0 + 0.15 * jax.random.normal(key_of[9], (D,), jnp.float32), 0.25, 1.75).astype(jnp.bfloat16),
        "slot_of": jax.vmap(lambda own: jax.random.permutation(own, SLOTS))(jax.random.split(key_of[10], GROUPS)).reshape((GROUPS, SLOTS)).astype(jnp.int32),
        "parent_of": draw_parent_of(jax.random.fold_in(key_of[13], 71), 0),
        "cotangent": centred(key_of[12], (TOKENS, D), 1.0, 6.0, ((0, 32),)),
    }


@jax.custom_vjp
def low(v):
    return lax.optimization_barrier(v.astype(jnp.bfloat16)).astype(jnp.float32)

@jax.custom_vjp
def low_back(v):
    return v

def low_keep(v):
    return (low(v), None)

def low_pass(kept, grad):
    return (grad,)

def back_keep(v):
    return (v, None)

def back_low(kept, grad):
    return (low(grad),)
low.defvjp(low_keep, low_pass)
low_back.defvjp(back_keep, back_low)
highest = lax.Precision.HIGHEST
norm_eps = 1e-05

def features(vectors):
    width = vectors.shape[-1]
    square = vectors[..., :, None] * vectors[..., None, :]
    square = square.reshape(vectors.shape[:-1] + (width * width,))
    return jnp.concatenate([jnp.ones_like(vectors[..., :1]), vectors / width ** 0.25, square / (math.sqrt(2.0) * math.sqrt(width))], axis=-1)

def rms_scale(values, gain):
    return values * lax.rsqrt(lax.optimization_barrier(jnp.mean(values * values, axis=-1, keepdims=True)) + norm_eps) * gain

def local_part(queries, key_heads, value_heads):
    length = queries.shape[1]
    scores = jnp.einsum('blhf,bmhf->bhlm', queries, key_heads, precision=highest) / math.sqrt(queries.shape[-1])
    scores = low_back(scores)
    row_index = lax.broadcasted_iota(jnp.int32, (length, length), 0)
    col_index = lax.broadcasted_iota(jnp.int32, (length, length), 1)
    kernel = jnp.where(col_index <= row_index, 1.0 + scores + 0.5 * scores * scores, 0.0)
    numerator = jnp.einsum('bhlm,bmhe->blhe', low(kernel), value_heads, precision=highest)
    denominator = jnp.einsum('bhlm->blh', kernel)
    return (numerator, denominator)

def family_forward(rows_in, params):
    query_weight, key_weight, value_weight, out_weight, gate_weight, up_weight, down_weight, attn_gain, mlp_gain = params
    length = rows_in.shape[0]
    hidden_one = low(rms_scale(rows_in, attn_gain))
    queries = low_back(low(jnp.dot(hidden_one, query_weight, precision=highest))).reshape(length, HEADS, FEAT)
    key_heads = low_back(low(jnp.dot(hidden_one, key_weight, precision=highest))).reshape(length, HEADS, FEAT)
    value_heads = low_back(low(jnp.dot(hidden_one, value_weight, precision=highest))).reshape(length, HEADS, DV)
    query_feat = low(features(queries))
    key_feat = low(features(key_heads))
    prompt_keys = key_feat[:PLEN].reshape(PIECES, TOK_DEV, HEADS, TAYLOR)
    prompt_values = value_heads[:PLEN].reshape(PIECES, TOK_DEV, HEADS, DV)
    value_state = jnp.einsum('pthe,pthf->phef', prompt_values, prompt_keys, precision=highest).reshape(PIECES, HEADS * DV, TAYLOR)
    norm_state = lax.optimization_barrier(jnp.sum(prompt_keys, axis=1))
    piece_states = low(low_back(jnp.concatenate([value_state, norm_state], axis=1)))
    before = (lax.broadcasted_iota(jnp.int32, (PIECES, PIECES), 1) < lax.broadcasted_iota(jnp.int32, (PIECES, PIECES), 0)).astype(jnp.float32)
    prefix = low(jnp.einsum('jp,prf->jrf', before, piece_states, precision=highest))
    whole = low(lax.optimization_barrier(jnp.sum(piece_states, axis=0)))
    prompt_query = query_feat[:PLEN].reshape(PIECES, TOK_DEV, HEADS, TAYLOR)
    prefix_values = prefix[:, :HEADS * DV].reshape(PIECES, HEADS, DV, TAYLOR)
    prefix_norms = prefix[:, HEADS * DV:]
    prompt_num = jnp.einsum('pthf,phef->pthe', prompt_query, prefix_values, precision=highest)
    prompt_den = jnp.einsum('pthf,phf->pth', prompt_query, prefix_norms, precision=highest)
    local_num, local_den = local_part(queries[:PLEN].reshape(PIECES, TOK_DEV, HEADS, FEAT), key_heads[:PLEN].reshape(PIECES, TOK_DEV, HEADS, FEAT), value_heads[:PLEN].reshape(PIECES, TOK_DEV, HEADS, DV))
    prompt_num = (prompt_num + local_num).reshape(PLEN, HEADS, DV)
    prompt_den = (prompt_den + local_den).reshape(PLEN, HEADS)
    cont_query = query_feat[PLEN:].reshape(CONT_PER, SEG, HEADS, TAYLOR)
    whole_values = whole[:HEADS * DV].reshape(HEADS, DV, TAYLOR)
    whole_norms = whole[HEADS * DV:]
    cont_num = jnp.einsum('cthf,hef->cthe', cont_query, whole_values, precision=highest)
    cont_den = jnp.einsum('cthf,hf->cth', cont_query, whole_norms, precision=highest)
    local_num, local_den = local_part(queries[PLEN:].reshape(CONT_PER, SEG, HEADS, FEAT), key_heads[PLEN:].reshape(CONT_PER, SEG, HEADS, FEAT), value_heads[PLEN:].reshape(CONT_PER, SEG, HEADS, DV))
    cont_num = (cont_num + local_num).reshape(PLEN, HEADS, DV)
    cont_den = (cont_den + local_den).reshape(PLEN, HEADS)
    numerator = low_back(jnp.concatenate([prompt_num, cont_num], axis=0))
    denominator = low_back(jnp.concatenate([prompt_den, cont_den], axis=0))
    mixed = low((numerator / denominator[:, :, None]).reshape(length, HEADS * DV))
    attn_out = low_back(jnp.dot(mixed, out_weight.T, precision=highest))
    after_attn = rows_in + attn_out
    hidden_two = low(rms_scale(after_attn, mlp_gain))
    gate_pre = low_back(jnp.dot(hidden_two, gate_weight, precision=highest))
    up_pre = low_back(jnp.dot(hidden_two, up_weight, precision=highest))
    activated = low(jax.nn.silu(gate_pre) * up_pre)
    return after_attn + jnp.dot(activated, down_weight.T, precision=highest)

def reference(inputs, query_weight, key_weight, value_weight, out_weight, gate_weight, up_weight, down_weight, attn_gain, mlp_gain, slot_of, parent_of, cotangent):
    dev_of_slot = jnp.argsort(slot_of, axis=1).astype(jnp.int32)
    cont_order = jnp.argsort(parent_of, axis=1, stable=True).astype(jnp.int32).reshape(GROUPS, FAMILIES, CONT_PER)
    piece_slot = (jnp.arange(FAMILIES, dtype=jnp.int32)[:, None] * PIECES + jnp.arange(PIECES, dtype=jnp.int32)[None, :]).reshape(-1)
    piece_dev = jnp.take(dev_of_slot, piece_slot, axis=1).reshape(GROUPS, FAMILIES, PIECES)
    prompt_rows = (piece_dev[..., None] * TOK_DEV + jnp.arange(TOK_DEV, dtype=jnp.int32)).reshape(GROUPS, FAMILIES, PLEN)
    pair_slot = (PIECE_SLOTS + cont_order // 2).reshape(GROUPS, FAMILIES * CONT_PER)
    cont_dev = jnp.take_along_axis(dev_of_slot, pair_slot, axis=1).reshape(GROUPS, FAMILIES, CONT_PER)
    cont_rows = (cont_dev[..., None] * TOK_DEV + (cont_order % 2)[..., None] * SEG + jnp.arange(SEG, dtype=jnp.int32)).reshape(GROUPS, FAMILIES, CONT_PER * SEG)
    group_base = (jnp.arange(GROUPS, dtype=jnp.int32) * (SLOTS * TOK_DEV))[:, None, None]
    flat_rows = (jnp.concatenate([prompt_rows, cont_rows], axis=2) + group_base).reshape(-1).astype(jnp.int32)
    rows_in = inputs.astype(jnp.float32)[flat_rows].reshape(GROUPS * FAMILIES, FAM_LEN, D)
    rows_cot = cotangent.astype(jnp.float32)[flat_rows].reshape(GROUPS * FAMILIES, FAM_LEN, D)
    params = tuple((weight_arg.astype(jnp.float32) for weight_arg in (query_weight, key_weight, value_weight, out_weight, gate_weight, up_weight, down_weight, attn_gain, mlp_gain)))

    def forward(all_rows, weights):
        return lax.map(lambda family_rows: jax.checkpoint(family_forward)(family_rows, weights), all_rows)
    outputs, pullback = jax.vjp(forward, rows_in, params)
    grad_rows, grad_params = pullback(rows_cot)
    block_out = jnp.zeros((TOKENS, D), jnp.float32).at[flat_rows].set(outputs.reshape(-1, D)).astype(jnp.bfloat16)
    input_grad = jnp.zeros((TOKENS, D), jnp.float32).at[flat_rows].set(grad_rows.reshape(-1, D))
    return (block_out, input_grad, grad_params[0], grad_params[1], grad_params[2], grad_params[3], grad_params[4], grad_params[5], grad_params[6], grad_params[7], grad_params[8])
```

```python
from functools import partial
import math

import jax
import jax.numpy as jnp
import numpy as np
from jax import lax
from jax.experimental import pallas as pl
from jax.experimental.pallas import tpu as pltpu
from jax.sharding import PartitionSpec as P

HEADS = 16
FEAT = 16
CONT_PER = 4
CHUNK = 256
FPAD = 256
FROWS = 160

norm_eps = 1e-05

f32 = jnp.float32
bf16 = jnp.bfloat16


def feature_table():
    table = np.zeros((8, FPAD), np.float32)
    table[0:2] = -1000.0
    table[2, 0] = table[3, 0] = table[4, 0] = table[5, 0] = 1.0
    at = 1
    for a in range(FEAT):
        table[0, at] = a
        table[3, at] = 1.0
        table[4, at] = table[5, at] = 0.5
        at += 1
    for a in range(FEAT):
        for b in range(a, FEAT):
            table[0, at] = a
            table[1, at] = b
            table[4, at] = 1.0 / (4.0 * math.sqrt(2.0))
            table[5, at] = table[4, at] * (1.0 if a == b else 2.0)
            at += 1
    return table


def mm(left, right):
    return lax.dot_general(left, right, (((1,), (0,)), ((), ())), preferred_element_type=f32)


def mm_nt(left, right):
    return lax.dot_general(left, right, (((1,), (1,)), ((), ())), preferred_element_type=f32)


def mm_tn(left, right):
    return lax.dot_general(left, right, (((0,), (0,)), ((), ())), preferred_element_type=f32)


def pick_rows(index_row, head, width):
    rows = lax.broadcasted_iota(jnp.int32, (width, FPAD), 0)
    return jnp.where(rows == index_row.astype(jnp.int32) + FEAT * head, 1.0, 0.0).astype(bf16)


def pick_cols(index_col, head, width):
    cols = lax.broadcasted_iota(jnp.int32, (FPAD, width), 1)
    return jnp.where(cols == index_col.astype(jnp.int32) + FEAT * head, 1.0, 0.0).astype(bf16)


def half_lanes(shape, half):
    lanes = lax.broadcasted_iota(jnp.int32, shape, len(shape) - 1)
    return ((lanes // 64) % 2) == half


def pair_join(first, second):
    return jnp.where(half_lanes(first.shape, 0), first, second)


def feats_t(tab, source_t, head):
    width = source_t.shape[0]
    first = mm(pick_cols(tab[:, 0:1], head, width), source_t) + tab[:, 2:3]
    second = mm(pick_cols(tab[:, 1:2], head, width), source_t) + tab[:, 3:4]
    return first * second


def state_kernel(flag_ref, tab_ref, kt_ref, v_ref, tot_ref, totz_ref, pre_ref, prez_ref):
    pair = pl.program_id(0)
    prompt = flag_ref[0].astype(f32)
    tab = tab_ref[...]
    chunks = v_ref.shape[0] // CHUNK
    sums = []
    feats = []
    for h in range(2):
        feats.append((feats_t(tab, kt_ref[...], 2 * pair + h) * tab[:, 4:5]).astype(bf16))
    for j in range(chunks):
        rows = slice(j * CHUNK, (j + 1) * CHUNK)
        values = v_ref[rows, :]
        ext = jnp.concatenate([values, jnp.ones_like(values)], axis=1)
        sums.append(pair_join(mm(feats[0][:, rows], ext), mm(feats[1][:, rows], ext)))
    first = sums[0] + sums[1]
    second = sums[2] + sums[3]
    total = first + second
    tot_ref[...] = total[:FROWS, :128].astype(bf16)
    lanes = lax.broadcasted_iota(jnp.int32, (FROWS, 128), 1)
    norms = total[:FROWS, 128:]
    shifted = jnp.where(
        lanes == 2 * pair,
        jnp.broadcast_to(norms[:, 0:1], norms.shape),
        jnp.where(lanes == 2 * pair + 1, jnp.broadcast_to(norms[:, 64:65], norms.shape), 0.0),
    ).astype(bf16)

    @pl.when(pair == 0)
    def _():
        totz_ref[...] = shifted

    @pl.when(pair > 0)
    def _():
        totz_ref[...] = totz_ref[...] + shifted

    prefix = [sums[0], first * prompt, first * prompt + sums[2]]
    for i in range(3):
        pre_ref[i] = prefix[i][:FROWS, :128].astype(bf16)
        prez_ref[i] = prefix[i][:FROWS, 128:].astype(bf16)


def running_states(pair, prompt, sin_ref, sinz_ref, pre_ref, prez_ref):
    lanes = lax.broadcasted_iota(jnp.int32, (128, 128), 0)
    wanted = 2 * pair + lax.broadcasted_iota(jnp.int32, (128, 128), 1) // 64
    spread = jnp.where(lanes == wanted, 1.0, 0.0).astype(bf16)
    base = []
    for n in range(2):
        norms = mm(sinz_ref[n], spread)
        base.append(jnp.concatenate([sin_ref[n].astype(f32), norms], axis=1))
    pad = jnp.zeros((FPAD - FROWS, 256), bf16)
    states = []
    for i in range(4):
        state = base[i // 2]
        if i >= 2:
            state = jnp.where(prompt > 0.5, base[0], base[1])
        if i >= 1:
            state = state + jnp.concatenate([pre_ref[i - 1], prez_ref[i - 1]], axis=1).astype(f32)
        states.append(jnp.concatenate([state.astype(bf16), pad], axis=0))
    return states


def head_lanes(head, shape):
    return (lax.broadcasted_iota(jnp.int32, shape, 1) // FEAT) == head


def causal(shape):
    return lax.broadcasted_iota(jnp.int32, shape, 1) <= lax.broadcasted_iota(jnp.int32, shape, 0)


def forward_kernel(
    flag_ref, tabr_ref, q_ref, kt_ref, v_ref, sin_ref, sinz_ref, pre_ref, prez_ref, y_ref, rden_ref
):
    pair = pl.program_id(0)
    prompt = flag_ref[0].astype(f32)
    tab = tabr_ref[...]
    states = running_states(pair, prompt, sin_ref, sinz_ref, pre_ref, prez_ref)
    width = q_ref.shape[1]
    allowed = causal((CHUNK, CHUNK))
    picks = [
        (pick_rows(tab[0:1], 2 * pair + h, width), pick_rows(tab[1:2], 2 * pair + h, width))
        for h in range(2)
    ]
    for i in range(4):
        rows = slice(i * CHUNK, (i + 1) * CHUNK)
        queries = q_ref[rows, :]
        values = v_ref[rows, :]
        ext = jnp.concatenate([values, jnp.ones_like(values)], axis=1)
        sums = []
        for h in range(2):
            head = 2 * pair + h
            masked = jnp.where(head_lanes(head, queries.shape), queries.astype(f32) * 0.25, 0.0)
            one_plus = mm(masked.astype(bf16), kt_ref[:, rows]) + 1.0
            kernel = jnp.where(allowed, 0.5 * one_plus * one_plus + 0.5, 0.0).astype(bf16)
            first = mm(queries, picks[h][0]) + tab[2:3]
            second = mm(queries, picks[h][1]) + tab[3:4]
            feats = (first * second * tab[5:6]).astype(bf16)
            sums.append(mm(kernel, ext) + mm(feats, states[i]))
        both = pair_join(sums[0], sums[1])
        rden = 1.0 / both[:, 128:]
        y_ref[rows, :] = (both[:, :128] * rden).astype(bf16)
        rden_ref[rows, :] = rden


def grad_state_kernel(
    flag_ref, tab_ref, qt_ref, dy_ref, y_ref, rden_ref,
    dnum_ref, dden_ref, tot_ref, totz_ref, suf_ref, sufz_ref,
):
    pair = pl.program_id(0)
    prompt = flag_ref[0].astype(f32)
    tab = tab_ref[...]
    rden = rden_ref[...]
    dy = dy_ref[...]
    prod = dy * y_ref[...].astype(f32)
    high = prod.astype(bf16)
    low = (prod - high.astype(f32)).astype(bf16)
    rows_half = (lax.broadcasted_iota(jnp.int32, (256, 128), 0) // 64) % 2
    lanes_half = lax.broadcasted_iota(jnp.int32, (256, 128), 1) // 64
    ones = jnp.where(rows_half == lanes_half, 1.0, 0.0).astype(bf16)
    total = mm(jnp.concatenate([high, low], axis=1), ones)
    dden = (-total * rden).astype(bf16)
    dnum = (dy * rden).astype(bf16)
    dnum_ref[...] = dnum
    dden_ref[...] = dden
    feats = []
    for h in range(2):
        feats.append((feats_t(tab, qt_ref[...], 2 * pair + h) * tab[:, 5:6]).astype(bf16))
    ext = jnp.concatenate([dnum, dden], axis=1)
    sums = []
    for i in range(4):
        rows = slice(i * CHUNK, (i + 1) * CHUNK)
        sums.append(pair_join(mm(feats[0][:, rows], ext[rows]), mm(feats[1][:, rows], ext[rows])))
    first = sums[0] + sums[1]
    second = sums[2] + sums[3]
    totals = [first + second * prompt, second * (1.0 - prompt)]
    lanes = lax.broadcasted_iota(jnp.int32, (FROWS, 128), 1)
    for n in range(2):
        tot_ref[n] = totals[n][:FROWS, :128].astype(bf16)
        norms = totals[n][:FROWS, 128:]
        shifted = jnp.where(
            lanes == 2 * pair,
            jnp.broadcast_to(norms[:, 0:1], norms.shape),
            jnp.where(lanes == 2 * pair + 1, jnp.broadcast_to(norms[:, 64:65], norms.shape), 0.0),
        ).astype(bf16)

        @pl.when(pair == 0)
        def _():
            totz_ref[n] = shifted

        @pl.when(pair > 0)
        def _():
            totz_ref[n] = totz_ref[n] + shifted

    suffix = [sums[1] + second * prompt, second * prompt, sums[3]]
    for i in range(3):
        suf_ref[i] = suffix[i][:FROWS, :128].astype(bf16)
        sufz_ref[i] = suffix[i][:FROWS, 128:].astype(bf16)


def backward_kernel(
    flag_ref, tab_ref, tabr_ref, q_ref, k_ref, kt_ref, v_ref, dnum_ref, dden_ref,
    sin_ref, sinz_ref, pre_ref, prez_ref, dp_ref, dpz_ref, suf_ref, sufz_ref,
    dq_ref, dk_ref, dv_ref, dq_acc, dk_acc,
):
    pair = pl.program_id(0)
    prompt = flag_ref[0].astype(f32)
    tabr = tabr_ref[...]
    tab = tab_ref[...]
    width = q_ref.shape[1]
    states = running_states(pair, prompt, sin_ref, sinz_ref, pre_ref, prez_ref)

    lanes = lax.broadcasted_iota(jnp.int32, (128, 128), 0)
    wanted = 2 * pair + lax.broadcasted_iota(jnp.int32, (128, 128), 1) // 64
    spread = jnp.where(lanes == wanted, 1.0, 0.0).astype(bf16)
    from_readers = jnp.concatenate([dp_ref[...].astype(f32), mm(dpz_ref[...], spread)], axis=1)
    pad = jnp.zeros((FPAD - FROWS, 256), bf16)
    grad_states = []
    for i in range(4):
        state = from_readers
        if i < 3:
            state = state + jnp.concatenate([suf_ref[i], sufz_ref[i]], axis=1).astype(f32)
        grad_states.append(jnp.concatenate([state.astype(bf16), pad], axis=0))

    allowed = causal((CHUNK, CHUNK))
    wide = lax.broadcasted_iota(jnp.int32, (CHUNK, 256), 1)

    @pl.when(pair == 0)
    def _():
        dq_acc[...] = jnp.zeros_like(dq_acc)
        dk_acc[...] = jnp.zeros_like(dk_acc)

    picks = []
    for h in range(2):
        head = 2 * pair + h
        picks.append(
            (
                pick_rows(tabr[0:1], head, width),
                pick_rows(tabr[1:2], head, width),
                pick_cols(tab[:, 0:1], head, width),
                pick_cols(tab[:, 1:2], head, width),
            )
        )
    for i in range(4):
        rows = slice(i * CHUNK, (i + 1) * CHUNK)
        queries = q_ref[rows, :]
        keys = k_ref[rows, :]
        values = v_ref[rows, :]
        ext = jnp.concatenate([values, jnp.ones_like(values)], axis=1)
        grads = jnp.concatenate([dnum_ref[rows, :], dden_ref[rows, :]], axis=1)
        dvs = []
        dq = None
        dk = None
        for h in range(2):
            head = 2 * pair + h
            mine = (wide // 64 == h) | (wide == 128 + 64 * h)
            in_head = head_lanes(head, queries.shape)
            q_head = jnp.where(in_head, queries.astype(f32) * 0.25, 0.0).astype(bf16)
            k_head = jnp.where(in_head, keys.astype(f32) * 0.25, 0.0).astype(bf16)
            grads_head = jnp.where(mine, grads, jnp.zeros_like(grads))
            ext_head = jnp.where(mine, ext, jnp.zeros_like(ext))
            one_plus = mm(q_head, kt_ref[:, rows]) + 1.0
            kernel = jnp.where(allowed, 0.5 * one_plus * one_plus + 0.5, 0.0).astype(bf16)
            dscore = jnp.where(allowed, mm_nt(grads_head, ext) * one_plus, 0.0).astype(bf16)
            pick_a, pick_b, back_a, back_b = picks[h]
            qa = mm(queries, pick_a) + tabr[2:3]
            qb = mm(queries, pick_b) + tabr[3:4]
            dfq = mm_nt(grads_head, states[i]) * tabr[5:6]
            ka = mm(keys, pick_a) + tabr[2:3]
            kb = mm(keys, pick_b) + tabr[3:4]
            fk = (ka * kb * tabr[4:5]).astype(bf16)
            dfk = mm_nt(ext_head, grad_states[i]) * tabr[4:5]
            dq_h = (
                mm(dscore, k_head)
                + mm((dfq * qb).astype(bf16), back_a)
                + mm((dfq * qa).astype(bf16), back_b)
            )
            dk_h = (
                mm_tn(dscore, q_head)
                + mm((dfk * kb).astype(bf16), back_a)
                + mm((dfk * ka).astype(bf16), back_b)
            )
            dq = dq_h if dq is None else dq + dq_h
            dk = dk_h if dk is None else dk + dk_h
            dvs.append(mm_tn(kernel, grads[:, :128]) + mm(fk, grad_states[i][:, :128]))
        dq_acc[rows, :] += dq
        dk_acc[rows, :] += dk
        dv_ref[rows, :] = pair_join(dvs[0], dvs[1]).astype(bf16)

    @pl.when(pair == pl.num_programs(0) - 1)
    def _():
        dq_ref[...] = dq_acc[...].astype(bf16)
        dk_ref[...] = dk_acc[...].astype(bf16)


def smem_spec():
    return pl.BlockSpec(memory_space=pltpu.SMEM)


def full_spec(shape):
    return pl.BlockSpec(shape, lambda p: (0,) * len(shape))


def lane_spec(shape):
    return pl.BlockSpec(shape, lambda p: (0,) * (len(shape) - 1) + (p,))


def shaped(shape, dtype):
    return jax.ShapeDtypeStruct(shape, dtype)


def cost(flops, moved):
    return pl.CostEstimate(flops=flops, bytes_accessed=moved, transcendentals=0)


PAIR_PASS = 2 * 256 * 256 * 256 * 4 * HEADS


def make_states(flag, table_t, keys_t, values):
    tok, width = values.shape
    pairs = width // 128
    return pl.pallas_call(
        state_kernel,
        grid=(pairs,),
        in_specs=[
            smem_spec(),
            full_spec((FPAD, 8)),
            full_spec(keys_t.shape),
            lane_spec((tok, 128)),
        ],
        out_specs=[
            lane_spec((FROWS, 128)),
            full_spec((FROWS, 128)),
            lane_spec((3, FROWS, 128)),
            lane_spec((3, FROWS, 128)),
        ],
        out_shape=[
            shaped((FROWS, width), bf16),
            shaped((FROWS, 128), bf16),
            shaped((3, FROWS, width), bf16),
            shaped((3, FROWS, width), bf16),
        ],
        cost_estimate=cost(3 * PAIR_PASS, 6 << 20),
        name="piece_states",
    )(flag, table_t, keys_t, values)


def attend(flag, table, queries, keys_t, values, states, norms, prefix, prefix_z):
    tok, width = values.shape
    return pl.pallas_call(
        forward_kernel,
        grid=(width // 128,),
        in_specs=[
            smem_spec(),
            full_spec((8, FPAD)),
            full_spec(queries.shape),
            full_spec(keys_t.shape),
            lane_spec((tok, 128)),
            lane_spec((2, FROWS, 128)),
            full_spec((2, FROWS, 128)),
            lane_spec((3, FROWS, 128)),
            lane_spec((3, FROWS, 128)),
        ],
        out_specs=[lane_spec((tok, 128)), lane_spec((tok, 128))],
        out_shape=[shaped((tok, width), bf16), shaped((tok, width), f32)],
        cost_estimate=cost(5 * PAIR_PASS, 14 << 20),
        name="attend_forward",
    )(flag, table, queries, keys_t, values, states, norms, prefix, prefix_z)


def grad_states_of(flag, table_t, queries_t, dy, mixed, rden):
    tok, width = mixed.shape
    return pl.pallas_call(
        grad_state_kernel,
        grid=(width // 128,),
        in_specs=[
            smem_spec(),
            full_spec((FPAD, 8)),
            full_spec(queries_t.shape),
            lane_spec((tok, 128)),
            lane_spec((tok, 128)),
            lane_spec((tok, 128)),
        ],
        out_specs=[
            lane_spec((tok, 128)),
            lane_spec((tok, 128)),
            lane_spec((2, FROWS, 128)),
            full_spec((2, FROWS, 128)),
            lane_spec((3, FROWS, 128)),
            lane_spec((3, FROWS, 128)),
        ],
        out_shape=[
            shaped((tok, width), bf16),
            shaped((tok, width), bf16),
            shaped((2, FROWS, width), bf16),
            shaped((2, FROWS, 128), bf16),
            shaped((3, FROWS, width), bf16),
            shaped((3, FROWS, width), bf16),
        ],
        cost_estimate=cost(3 * PAIR_PASS, 18 << 20),
        name="state_gradients",
    )(flag, table_t, queries_t, dy, mixed, rden)


def attend_backward(
    flag, table_t, table, queries, keys, keys_t, values, dnum, dden,
    states, norms, prefix, prefix_z, dp, dpz, suffix, suffix_z,
):
    tok, width = values.shape
    qk = queries.shape[1]
    return pl.pallas_call(
        backward_kernel,
        grid=(width // 128,),
        in_specs=[
            smem_spec(),
            full_spec((FPAD, 8)),
            full_spec((8, FPAD)),
            full_spec(queries.shape),
            full_spec(keys.shape),
            full_spec(keys_t.shape),
            lane_spec((tok, 128)),
            lane_spec((tok, 128)),
            lane_spec((tok, 128)),
            lane_spec((2, FROWS, 128)),
            full_spec((2, FROWS, 128)),
            lane_spec((3, FROWS, 128)),
            lane_spec((3, FROWS, 128)),
            lane_spec((FROWS, 128)),
            full_spec((FROWS, 128)),
            lane_spec((3, FROWS, 128)),
            lane_spec((3, FROWS, 128)),
        ],
        out_specs=[full_spec((tok, qk)), full_spec((tok, qk)), lane_spec((tok, 128))],
        out_shape=[
            shaped((tok, qk), bf16),
            shaped((tok, qk), bf16),
            shaped((tok, width), bf16),
        ],
        scratch_shapes=[pltpu.VMEM((tok, qk), f32), pltpu.VMEM((tok, qk), f32)],
        cost_estimate=cost(16 * PAIR_PASS, 16 << 20),
        name="attend_backward",
    )(
        flag, table_t, table, queries, keys, keys_t, values, dnum, dden,
        states, norms, prefix, prefix_z, dp, dpz, suffix, suffix_z,
    )


def gather_rows(part):
    return lax.all_gather(part, "shard", axis=0, tiled=True)


def reduce_rows(grad):
    share = lax.psum_scatter(grad.astype(bf16), "shard", scatter_dimension=0, tiled=True)
    return lax.psum(share, "rep").astype(f32)


def local(
    inputs,
    query_weight,
    key_weight,
    value_weight,
    out_weight,
    gate_weight,
    up_weight,
    down_weight,
    attn_gain,
    mlp_gain,
    slot_of,
    parent_of,
    cotangent,
):
    tok_rows, width = inputs.shape
    qk_width = query_weight.shape[1]
    value_width = value_weight.shape[1]
    shards = lax.axis_size("shard")
    own_index = lax.axis_index("shard")
    slot_ids = slot_of[0]
    parent_ids = parent_of[0]
    prompt_slots = shards // 2
    pieces_per = CONT_PER // 2
    own_slot = lax.dynamic_index_in_dim(slot_ids, own_index, keepdims=False)
    own_prompt = own_slot < prompt_slots
    source_prompt = slot_ids < prompt_slots
    source_family = slot_ids // pieces_per
    earlier = (
        source_prompt
        & (source_family == own_slot // pieces_per)
        & (slot_ids % pieces_per < own_slot % pieces_per)
    )
    pair_index = jnp.clip(own_slot - prompt_slots, 0, shards // 2 - 1)
    first_parent = lax.dynamic_index_in_dim(parent_ids, 2 * pair_index, keepdims=False)
    second_parent = lax.dynamic_index_in_dim(parent_ids, 2 * pair_index + 1, keepdims=False)
    from_first = source_prompt & (source_family == first_parent)
    from_second = source_prompt & (source_family == second_parent)
    source_mix = jnp.where(
        own_prompt, jnp.stack([earlier, earlier]), jnp.stack([from_first, from_second])
    ).astype(f32)
    flag = own_prompt.astype(jnp.int32).reshape(1)
    table_np = feature_table()
    table = jnp.asarray(table_np)
    table_t = jnp.asarray(np.ascontiguousarray(table_np.T))

    gains = jnp.zeros((attn_gain.shape[0], 128), bf16)
    gains = gains.at[:, 0].set(attn_gain).at[:, 1].set(mlp_gain)
    packed = gather_rows(jnp.concatenate([query_weight, key_weight, value_weight, gains], axis=1))
    qkv_width = 2 * qk_width + value_width
    qkv_weight = packed[:, :qkv_width]
    gain_one = packed[:, qkv_width].astype(f32)[None]
    gain_two = packed[:, qkv_width + 1].astype(f32)[None]
    out_full = gather_rows(out_weight)
    down_full = gather_rows(down_weight)
    gate_full = gather_rows(gate_weight)
    up_full = gather_rows(up_weight)

    x = inputs.astype(f32)
    inv_one = lax.rsqrt(jnp.mean(x * x, axis=1, keepdims=True) + norm_eps)
    norm_one = x * inv_one
    hidden_one = (norm_one * gain_one).astype(bf16)
    qkv = mm(hidden_one, qkv_weight).astype(bf16)
    queries = qkv[:, :qk_width]
    keys = qkv[:, qk_width : 2 * qk_width]
    values = qkv[:, 2 * qk_width :]
    queries_t = queries.T
    keys_t = keys.T

    total, total_z, prefix, prefix_z = make_states(flag, table_t, keys_t, values)
    own_state = jnp.concatenate([total, total_z], axis=1)
    all_states = lax.all_gather(own_state, "shard", axis=0, tiled=False)
    used = jnp.einsum(
        "sn,nfl->sfl", source_mix.astype(bf16), all_states, preferred_element_type=f32
    ).astype(bf16)
    used_states = used[:, :, :value_width]
    used_norms = used[:, :, value_width:]
    mixed, rden = attend(
        flag, table, queries, keys_t, values, used_states, used_norms, prefix, prefix_z
    )

    after_attn = x + mm_nt(mixed, out_full)
    inv_two = lax.rsqrt(jnp.mean(after_attn * after_attn, axis=1, keepdims=True) + norm_eps)
    norm_two = after_attn * inv_two
    hidden_two = (norm_two * gain_two).astype(bf16)
    gate_pre = mm(hidden_two, gate_full)
    up_pre = mm(hidden_two, up_full)
    sigma = jax.nn.sigmoid(gate_pre)
    activated = (gate_pre * sigma * up_pre).astype(bf16)
    grad_act = mm(cotangent, down_full)
    down_grad = reduce_rows(mm_tn(cotangent, activated))
    grad_up = (grad_act * gate_pre * sigma).astype(bf16)
    grad_gate = (grad_act * up_pre * sigma * (1.0 + gate_pre * (1.0 - sigma))).astype(bf16)
    up_grad = reduce_rows(mm_tn(hidden_two, grad_up))
    gate_grad = reduce_rows(mm_tn(hidden_two, grad_gate))
    block_out = (after_attn + mm_nt(activated, down_full)).astype(bf16)

    grad_hidden_two = mm_nt(grad_gate, gate_full) + mm_nt(grad_up, up_full)
    grad_norm_two = grad_hidden_two * gain_two
    grad_after = cotangent.astype(f32) + inv_two * (
        grad_norm_two - norm_two * jnp.mean(grad_norm_two * norm_two, axis=1, keepdims=True)
    )
    grad_attn = grad_after.astype(bf16)
    out_grad = reduce_rows(mm_tn(grad_attn, mixed))
    dy = mm(grad_attn, out_full)
    dnum, dden, dstate, dstate_z, suffix, suffix_z = grad_states_of(
        flag, table_t, queries_t, dy, mixed, rden
    )
    grad_slots = jnp.concatenate([dstate, dstate_z], axis=2)
    to_sources = jnp.einsum(
        "sn,sfl->nfl", source_mix.astype(bf16), grad_slots, preferred_element_type=f32
    ).astype(bf16)
    grad_piece = lax.psum_scatter(to_sources, "shard", scatter_dimension=0, tiled=False)
    dq, dk, dv = attend_backward(
        flag, table_t, table, queries, keys, keys_t, values, dnum, dden,
        used_states, used_norms, prefix, prefix_z,
        grad_piece[:, :value_width], grad_piece[:, value_width:], suffix, suffix_z,
    )
    grad_qkv = jnp.concatenate([dq, dk, dv], axis=1)
    grad_hidden_one = mm_nt(grad_qkv, qkv_weight)
    grad_norm_one = grad_hidden_one * gain_one
    input_grad = grad_after + inv_one * (
        grad_norm_one - norm_one * jnp.mean(grad_norm_one * norm_one, axis=1, keepdims=True)
    )
    gain_grads = jnp.stack(
        [
            jnp.sum(grad_hidden_one * norm_one, axis=0),
            jnp.sum(grad_hidden_two * norm_two, axis=0),
        ],
        axis=1,
    )
    last = reduce_rows(
        jnp.concatenate(
            [
                mm_tn(hidden_one, grad_qkv).astype(bf16),
                jnp.pad(gain_grads, ((0, 0), (0, 126))).astype(bf16),
            ],
            axis=1,
        )
    )
    return (
        block_out,
        input_grad,
        last[:, :qk_width],
        last[:, qk_width : 2 * qk_width],
        last[:, 2 * qk_width : qkv_width],
        out_grad,
        gate_grad,
        up_grad,
        down_grad,
        last[:, qkv_width],
        last[:, qkv_width + 1],
    )


def solution(mesh):
    placed = (P(("rep", "shard"), None),) + (P("shard", None),) * 7 + (P("shard"),) * 2
    placed = placed + (P("rep", None),) * 2 + (P(("rep", "shard"), None),)
    return jax.shard_map(
        local,
        mesh=mesh,
        in_specs=placed,
        out_specs=(P(("rep", "shard"), None),) * 2
        + (P("shard", None),) * 7
        + (P("shard"),) * 2,
        check_vma=False,
    )
```
